512 devices in a mesh: row: 16 (over x, y_lo), col: 32 (over y_hi, z, core).
Axes of the slice: x: 4, y: 8 (y_hi: 2, y_lo: 4; y = y_hi * 4 + y_lo), z: 8, core: 2. Of those that a mesh axis runs over, the one named last changes fastest.
Arguments:
- row_ids: int32 [128], P('row'), may hold values from -1 to 127, as said below
- a_tiles: bfloat16 [8192, 4096], P('row', 'col'), may hold values from -6 to 6
- a_mask: int32 [128, 64], P('row', 'col'), may hold values 0 or 1
- b_tiles: bfloat16 [4096, 24576], P('row', 'col'), may hold values from -0.1875 to 0.1875
- b_mask: int32 [64, 384], P('row', 'col'), may hold values 0 or 1
- c_keep: int32 [128, 384], P(None, 'col'), may hold values 0 or 1
Outputs:
- product_out: bfloat16 [8192, 24576], P('row', 'col')
The draws below stay inside these ranges and needn't reach their ends.
Inputs may be any that keep to these rules, and one draw needn't show every extreme that they name: `row_ids`: within a group of 8 slots the live ids come first and -1 fills the rest; live ids are distinct over all slots; every group has at least half of its slots live and some group has all 8 live.
All inputs are finite; a program needn't handle non-finite values. No bound on the sum of `a_mask` or of `b_mask` or of `c_keep` on one device may be relied on, other than what follows from the above.
Results may differ from the reference program's by a relative error of at most 0.001.
Values may be sent and summed in bfloat16 or wider, within the bound.
A program may use at most 64 MiB of HBM per device.

```python
import jax
import jax.numpy as jnp
from jax import lax

TILE = 64
KB = 2
CB = 12
S = 8
GROUPS = 16
PANELS = 32


def draw_row_ids(key, part):
    first_key, second_key, third_key = jax.random.split(key, 3)
    counts = jax.random.randint(first_key, (GROUPS,), (S + 1) // 2, S + 1)
    full_group = jax.random.randint(second_key, (), 0, GROUPS)
    counts = jnp.where(jnp.arange(GROUPS, dtype=jnp.int32) == full_group, S, counts)
    shuffled = jax.random.permutation(third_key, GROUPS * S).astype(jnp.int32)
    positions = jnp.arange(GROUPS * S, dtype=jnp.int32)
    within = positions % S
    owner = positions // S
    return jnp.where(within < counts[owner], shuffled, -1).astype(jnp.int32)


def set_ends(array, key, least, largest):
    place = [jax.random.randint(jax.random.fold_in(key, axis), (), 0, length) for axis, length in enumerate(array.shape)]
    longest = array.shape.index(max(array.shape))
    neighbour = place[:longest] + [(place[longest] + 1) % array.shape[longest]] + place[longest + 1:]
    return array.at[tuple(place)].set(least).at[tuple(neighbour)].set(largest)


def block_scale(stream_key, dims, cuts, low, high):
    loudness = 1.0
    for position, parts in cuts:
        heights = jax.random.uniform(jax.random.fold_in(jax.random.fold_in(stream_key, 6), position), (parts,), jnp.float32, low / len(cuts), high / len(cuts))
        loudness = loudness * jnp.repeat(jnp.exp(heights), dims[position] // parts).reshape((-1,) + (1,) * (len(dims) - 1 - position))
    return loudness


def normal_values(key, dims, width, limit, cuts=(), kind=jnp.bfloat16):
    array = width * jax.random.normal(key, dims, jnp.float32)
    if cuts:
        array = array * block_scale(key, dims, cuts, -0.22, 0.18)
    return jnp.clip(array, -limit, limit).astype(kind)


def setup_inputs(seed: int = 0) -> dict:
    key_list = jax.random.split(jax.random.key(seed), 7)
    return {
        "row_ids": draw_row_ids(jax.random.fold_in(key_list[6], 71), 0),
        "a_tiles": normal_values(key_list[1], (GROUPS * S * TILE, PANELS * KB * TILE), 1.0, 6.0, ((0, 16), (1, 32))),
        "a_mask": set_ends((jax.random.randint(key_list[2], (GROUPS * S, PANELS * KB), 0, 2) < 1).astype(jnp.int32), jax.random.fold_in(key_list[2], 1), 0, 1),
        "b_tiles": normal_values(key_list[3], (PANELS * KB * TILE, PANELS * CB * TILE), (PANELS * KB * TILE // 4) ** -0.5, 0.1875, ((0, 16), (1, 32))),
        "b_mask": set_ends((jax.random.randint(key_list[4], (PANELS * KB, PANELS * CB), 0, 2) < 1).astype(jnp.int32), jax.random.fold_in(key_list[4], 1), 0, 1),
        "c_keep": set_ends((jax.random.randint(key_list[5], (GROUPS * S, PANELS * CB), 0, 4) < 3).astype(jnp.int32), jax.random.fold_in(key_list[5], 1), 0, 1),
    }


def reference(row_ids, a_tiles, a_mask, b_tiles, b_mask, c_keep):
    ratio_cols = PANELS // GROUPS
    panel_width = KB * TILE
    a_masked = a_tiles.reshape(GROUPS * S, TILE, PANELS * KB, TILE) * a_mask.astype(jnp.bfloat16)[:, None, :, None]
    a_masked = a_masked.reshape(GROUPS, S * TILE, PANELS, panel_width)
    b_masked = b_tiles.reshape(PANELS * KB, TILE, PANELS * CB, TILE) * b_mask.astype(jnp.bfloat16)[:, None, :, None]
    b_masked = b_masked.reshape(PANELS, panel_width, PANELS, CB * TILE)
    col_shift = jnp.arange(PANELS, dtype=jnp.int32)
    b_inner = jax.vmap(lambda block_cols, shift_by: jnp.roll(block_cols, shift_by, axis=0), in_axes=(2, 0), out_axes=2)(b_masked, col_shift)
    b_inner = b_inner.reshape(PANELS * panel_width, PANELS * CB * TILE)
    clipped = jnp.maximum(row_ids, 0).astype(jnp.int32)
    keep = jnp.where(row_ids[:, None] >= 0, c_keep[clipped].astype(jnp.float32), jnp.zeros((), jnp.float32))
    keep = keep.reshape(GROUPS, S, PANELS * CB)

    def one_group(inputs):
        group_rows, group_index, group_keep = inputs
        a_inner = jnp.roll(group_rows, ratio_cols * group_index + ratio_cols - 1, axis=1)
        a_inner = a_inner.reshape(S * TILE, PANELS * panel_width)
        product = jnp.dot(a_inner, b_inner, preferred_element_type=jnp.float32)
        masked = product.reshape(S, TILE, PANELS * CB, TILE) * group_keep[:, None, :, None]
        return masked.reshape(S * TILE, PANELS * CB * TILE).astype(jnp.bfloat16)

    result = lax.map(one_group, (a_masked, jnp.arange(GROUPS, dtype=jnp.int32), keep))
    return result.reshape(GROUPS * S * TILE, PANELS * CB * TILE)
```

```python
import jax
import jax.numpy as jnp
from jax import lax
from jax.experimental import pallas as pl
from jax.experimental.pallas import tpu as pltpu
from jax.sharding import PartitionSpec as P

TILE = 64
NX, NY, NH, NZ = 4, 4, 2, 8
MESH = pl.DeviceIdType.MESH


def kernel(a_ref, b_ref, out_ref, a_all, b_all, acc, a_recv, b_recv, core_send, z_send, h_send,
           y_send, x_send, f_send):
    row = lax.axis_index("row")
    col = lax.axis_index("col")
    x, y = row // NY, row % NY
    core, z, h = col % 2, (col // 2) % NZ, col // (2 * NZ)

    def row_at(xi, yi):
        return xi * NY + yi

    def col_at(hi, zi, ci):
        return (hi * NZ + zi) * 2 + ci

    x_next, x_prev, x_far = (x + 1) % NX, (x + NX - 1) % NX, (x + 2) % NX
    to_x = ((row_at(x_next, y), col), (row_at(x_prev, y), col))
    to_y = ((row_at(x, (y + 1) % NY), col), (row_at(x, (y + NY - 1) % NY), col))
    to_z = ((row, col_at(h, (z + 1) % NZ, core)), (row, col_at(h, (z + NZ - 1) % NZ, core)))
    to_core = (row, col_at(h, z, 1 - core))
    to_h = (row, col_at(1 - h, z, core))

    barrier = pltpu.get_barrier_semaphore()
    partners = (*to_x, *to_y, *to_z, to_core, to_h)
    for partner in partners:
        pl.semaphore_signal(barrier, inc=1, device_id=partner, device_id_type=MESH)
    pl.semaphore_wait(barrier, len(partners))

    def a_copy(source, q, send, to):
        return pltpu.make_async_remote_copy(
            src_ref=source, dst_ref=a_all.at[q], send_sem=send, recv_sem=a_recv.at[q],
            device_id=to, device_id_type=MESH)

    def b_copy(source, panel, send, to):
        return pltpu.make_async_remote_copy(
            src_ref=source, dst_ref=b_all.at[panel], send_sem=send, recv_sem=b_recv.at[panel],
            device_id=to, device_id_type=MESH)

    def a_arrived(q):
        a_copy(a_all.at[q], q, core_send.at[0], to_core).wait_recv()

    def b_arrived(panel):
        b_copy(b_all.at[panel], panel, x_send.at[0, 0, 0], to_x[0]).wait_recv()

    def panel_at(xi, yi, p):
        return row_at(xi, yi) * 2 + p

    def own_b(p):
        return b_ref.at[pl.ds(p * 128, 128)]

    def y_copy(source, yi, p, way):
        return b_copy(source, panel_at(x, yi, p), y_send.at[way, yi, p], to_y[way])

    def x_copy(source, yi, p, way):
        return b_copy(source, panel_at(x, yi, p), x_send.at[way, yi, p], to_x[way])

    a_hops = ((4, 3), (3, 4))

    def z_copy(source, q, kind, way, hop):
        return a_copy(source, q, z_send.at[kind, way, hop], to_z[way])

    def core_copy(source, q, zi, kind):
        return a_copy(source, q, core_send.at[kind * NZ + zi], to_core)

    a_copy(a_ref, col, h_send, to_h).start()
    z_copy(a_ref, col, 0, 0, 0).start()
    z_copy(a_ref, col, 0, 1, 0).start()
    for p in (0, 1):
        @pl.when(y < NY - 1)
        def _(p=p):
            y_copy(own_b(p), y, p, 0).start()

        @pl.when(y > 0)
        def _(p=p):
            y_copy(own_b(p), y, p, 1).start()

        x_copy(own_b(p), y, p, 0).start()
        x_copy(own_b(1 - p), y, 1 - p, 1).start()
    core_copy(a_ref, col, z, 0).start()

    a_all[col] = a_ref[...]
    b_all[row * 2] = b_ref[:128]
    b_all[row * 2 + 1] = b_ref[128:]
    acc[...] = jnp.zeros_like(acc)

    def a_step(kind, step):
        half = h if kind == 0 else 1 - h
        for way in (0, 1):
            if step <= a_hops[kind][way]:
                zi = (z + (NZ - step if way == 0 else step)) % NZ
                q = col_at(half, zi, core)
                a_arrived(q)
                if step < a_hops[kind][way]:
                    z_copy(a_all.at[q], q, kind, way, step).start()
                core_copy(a_all.at[q], q, zi, kind).start()

    def a_other_half():
        q = col_at(1 - h, z, core)
        a_arrived(q)
        z_copy(a_all.at[q], q, 1, 0, 0).start()
        z_copy(a_all.at[q], q, 1, 1, 0).start()
        core_copy(a_all.at[q], q, z, 1).start()

    def y_step(step):
        for way in (0, 1):
            yi = y - step if way == 0 else y + step

            @pl.when((yi >= 0) & (yi < NY))
            def _(yi=yi, way=way):
                for p in (0, 1):
                    panel = panel_at(x, yi, p)
                    b_arrived(panel)

                    @pl.when((y < NY - 1) if way == 0 else (y > 0))
                    def _():
                        y_copy(b_all.at[panel], yi, p, way).start()

                    x_copy(b_all.at[panel], yi, p, 0).start()
                    x_copy(b_all.at[panel], yi, p, 1).start()

    order = (
        y,
        jnp.where(y == 0, 1, y - 1),
        jnp.where(y <= 1, 2, jnp.where(y == 2, 3, 1)),
        jnp.where(y <= 1, 3, 0),
    )

    def f_copy(k, way):
        panel = panel_at(x_prev if way == 0 else x_next, order[k], way)
        return b_copy(b_all.at[panel], panel, f_send.at[way, k], to_x[way])

    def x_forward(k):
        b_arrived(panel_at(x_prev, order[k], 0))
        f_copy(k, 0).start()
        b_arrived(panel_at(x_next, order[k], 1))
        f_copy(k, 1).start()

    def multiply(k):
        yi = order[k]
        b_arrived(panel_at(x_prev, yi, 1))
        b_arrived(panel_at(x_next, yi, 0))
        b_arrived(panel_at(x_far, yi, 0))
        b_arrived(panel_at(x_far, yi, 1))

        @pl.loop(0, NX)
        def _(xi):
            first = row_at(xi, yi) * 2
            shift = first + col + 64 - 2 * row - 1
            a_two = jnp.concatenate([a_all[shift % 32], a_all[(shift + 1) % 32]], axis=1)
            for n in range(3):
                cols = pl.ds(n * 256, 256)
                b_two = jnp.concatenate([b_all[first, :, cols], b_all[first + 1, :, cols]], axis=0)
                acc[:, cols] += jnp.dot(a_two, b_two, preferred_element_type=jnp.float32)

    a_step(0, 1)
    y_step(1)
    x_forward(0)
    a_other_half()
    a_step(0, 2)
    a_step(1, 1)
    y_step(2)
    x_forward(1)
    a_step(0, 3)
    a_step(1, 2)
    y_step(3)
    a_step(0, 4)
    a_step(1, 3)
    x_forward(2)
    a_step(1, 4)
    for half in range(NH):
        for zi in range(NZ):
            a_arrived(col_at(half, zi, 1 - core))
    multiply(0)
    multiply(1)
    x_forward(3)
    multiply(2)
    multiply(3)
    out_ref[...] = acc[...].astype(out_ref.dtype)

    a_copy(a_ref, col, h_send, to_h).wait_send()
    for kind in (0, 1):
        for way in (0, 1):
            for hop in range(a_hops[kind][way]):
                z_copy(a_ref, col, kind, way, hop).wait_send()
        for zi in range(NZ):
            core_copy(a_ref, col, zi, kind).wait_send()
    for p in (0, 1):
        for yi in range(NY):
            @pl.when((y < NY - 1) & (yi <= y))
            def _(yi=yi, p=p):
                y_copy(own_b(p), yi, p, 0).wait_send()

            @pl.when((y > 0) & (yi >= y))
            def _(yi=yi, p=p):
                y_copy(own_b(p), yi, p, 1).wait_send()

            for way in (0, 1):
                x_copy(own_b(p), yi, p, way).wait_send()
    for k in range(NY):
        for way in (0, 1):
            f_copy(k, way).wait_send()


def per_device(row_ids, a_tiles, a_mask, b_tiles, b_mask, c_keep):
    def by_blocks(array, blocks):
        wide = jnp.repeat(blocks, TILE, axis=1).astype(array.dtype)
        tall = array.reshape(blocks.shape[0], TILE, array.shape[1])
        return (tall * wide[:, None, :]).reshape(array.shape)

    a_eff = by_blocks(a_tiles, a_mask)
    b_eff = by_blocks(b_tiles, b_mask)
    dma = pltpu.SemaphoreType.DMA
    product = pl.pallas_call(
        kernel,
        out_shape=jax.ShapeDtypeStruct((512, 768), jnp.bfloat16),
        in_specs=[pl.BlockSpec(memory_space=pltpu.VMEM)] * 2,
        out_specs=pl.BlockSpec(memory_space=pltpu.VMEM),
        scratch_shapes=[
            pltpu.VMEM((32, 512, 128), jnp.bfloat16),
            pltpu.VMEM((32, 128, 768), jnp.bfloat16),
            pltpu.VMEM((512, 768), jnp.float32),
            dma((32,)),
            dma((32,)),
            dma((16,)),
            dma((2, 2, 4)),
            dma,
            dma((2, NY, 2)),
            dma((2, NY, 2)),
            dma((2, NY)),
        ],
        compiler_params=pltpu.CompilerParams(collective_id=0, has_side_effects=True),
    )(a_eff, b_eff)
    onehot = (row_ids[:, None] == jnp.arange(c_keep.shape[0], dtype=jnp.int32)[None, :]).astype(
        jnp.float32
    )
    keep = jnp.dot(onehot, c_keep.astype(jnp.float32))
    return by_blocks(product, keep)


def solution(mesh):
    placed = (
        P("row"),
        P("row", "col"),
        P("row", "col"),
        P("row", "col"),
        P("row", "col"),
        P(None, "col"),
    )
    return jax.shard_map(
        per_device, mesh=mesh, in_specs=placed, out_specs=P("row", "col"), check_vma=False
    )
```

```python
import jax
import jax.numpy as jnp
from jax import lax
from jax.experimental import pallas as pl
from jax.experimental.pallas import tpu as pltpu
from jax.sharding import PartitionSpec as P

TILE = 64
NX, NY, NH, NZ = 4, 4, 2, 8
MAIN, EDGE = 112, 16
MESH = pl.DeviceIdType.MESH


def kernel(a_ref, b_ref, out_ref, a_all, b_all, acc, a_recv, b_recv, e_recv, u_recv, core_send, z_send,
           h_send, y_send, x_send, f_send, e_send, ef_send, u_send, local_sem):
    row = lax.axis_index("row")
    col = lax.axis_index("col")
    x, y = row // NY, row % NY
    core, z, h = col % 2, (col // 2) % NZ, col // (2 * NZ)

    def row_at(xi, yi):
        return xi * NY + yi

    def col_at(hi, zi, ci):
        return (hi * NZ + zi) * 2 + ci

    x_next, x_prev, x_far = (x + 1) % NX, (x + NX - 1) % NX, (x + 2) % NX
    to_x = ((row_at(x_next, y), col), (row_at(x_prev, y), col))
    to_y = ((row_at(x, (y + 1) % NY), col), (row_at(x, (y + NY - 1) % NY), col))
    to_z = ((row, col_at(h, (z + 1) % NZ, core)), (row, col_at(h, (z + NZ - 1) % NZ, core)))
    to_core = (row, col_at(h, z, 1 - core))
    to_h = (row, col_at(1 - h, z, core))

    barrier = pltpu.get_barrier_semaphore()
    partners = (*to_x, *to_y, *to_z, to_core, to_h)
    for partner in partners:
        pl.semaphore_signal(barrier, inc=1, device_id=partner, device_id_type=MESH)
    pl.semaphore_wait(barrier, len(partners))

    def send(source, target, send_sem, recv_sem, to):
        return pltpu.make_async_remote_copy(
            src_ref=source, dst_ref=target, send_sem=send_sem, recv_sem=recv_sem,
            device_id=to, device_id_type=MESH)

    def arrived(target, recv_sem):
        send(target, target, h_send, recv_sem, to_core).wait_recv()

    def a_copy(source, q, send_sem, to):
        return send(source, a_all.at[q], send_sem, a_recv.at[q], to)

    def a_arrived(q):
        arrived(a_all.at[q], a_recv.at[q])

    def main(xi, yi, p):
        return b_all.at[xi, yi, pl.ds(p * MAIN, MAIN)]

    def edge(xi, yi, p):
        return b_all.at[xi, yi, pl.ds(2 * MAIN + p * EDGE, EDGE)]

    def bundle(yi):
        return b_all.at[:, yi, pl.ds(2 * MAIN, 2 * EDGE)]

    def main_copy(source, xi, yi, p, send_sem, to):
        return send(source, main(xi, yi, p), send_sem, b_recv.at[xi, yi, p], to)

    def main_arrived(xi, yi, p):
        arrived(main(xi, yi, p), b_recv.at[xi, yi, p])

    def edge_arrived(xi, p):
        arrived(edge(xi, y, p), e_recv.at[xi, p])

    def own_main(p):
        return b_ref.at[pl.ds(p * MAIN, MAIN)]

    def own_edge(p):
        return b_ref.at[pl.ds(2 * MAIN + p * EDGE, EDGE)]

    def y_copy(source, yi, p, way):
        return main_copy(source, x, yi, p, y_send.at[way, yi, p], to_y[way])

    def x_copy(source, yi, p, way):
        return main_copy(source, x, yi, p, x_send.at[way, yi, p], to_x[way])

    def e_copy(p, way):
        return send(own_edge(p), edge(x, y, p), e_send.at[way, p], e_recv.at[x, p], to_x[way])

    def e_forward(way):
        xi = x_prev if way == 0 else x_next
        return send(edge(xi, y, way), edge(xi, y, way), ef_send.at[way], e_recv.at[xi, way], to_x[way])

    def u_copy(yi, way):
        return send(bundle(yi), bundle(yi), u_send.at[way, yi], u_recv.at[yi], to_y[way])

    a_hops = ((4, 3), (3, 4))

    def z_copy(source, q, kind, way, hop):
        return a_copy(source, q, z_send.at[kind, way, hop], to_z[way])

    def core_copy(source, q, zi, kind):
        return a_copy(source, q, core_send.at[kind * NZ + zi], to_core)

    def further(way):
        return (y < NY - 1) if way == 0 else (y > 0)

    for p in (0, 1):
        e_copy(p, 0).start()
        e_copy(1 - p, 1).start()
    for p in (0, 1):
        for way in (0, 1):
            @pl.when(further(way))
            def _():
                y_copy(own_main(p), y, p, way).start()

        x_copy(own_main(p), y, p, 0).start()
        x_copy(own_main(1 - p), y, 1 - p, 1).start()
    z_copy(a_ref, col, 0, 0, 0).start()
    z_copy(a_ref, col, 0, 1, 0).start()
    a_copy(a_ref, col, h_send, to_h).start()
    core_copy(a_ref, col, z, 0).start()
    local = pltpu.make_async_copy(b_ref, b_all.at[x, y], local_sem)
    local.start()

    a_all[col] = a_ref[...]
    acc[...] = jnp.zeros_like(acc)

    def a_step(kind, step):
        half = h if kind == 0 else 1 - h
        for way in (0, 1):
            if step <= a_hops[kind][way]:
                zi = (z + (NZ - step if way == 0 else step)) % NZ
                q = col_at(half, zi, core)
                a_arrived(q)
                if step < a_hops[kind][way]:
                    z_copy(a_all.at[q], q, kind, way, step).start()
                core_copy(a_all.at[q], q, zi, kind).start()

    def a_other_half():
        q = col_at(1 - h, z, core)
        a_arrived(q)
        z_copy(a_all.at[q], q, 1, 0, 0).start()
        z_copy(a_all.at[q], q, 1, 1, 0).start()
        core_copy(a_all.at[q], q, z, 1).start()

    def y_step(step):
        for way in (0, 1):
            yi = y - step if way == 0 else y + step

            @pl.when((yi >= 0) & (yi < NY))
            def _(yi=yi, way=way):
                for p in (0, 1):
                    main_arrived(x, yi, p)

                    @pl.when(further(way))
                    def _():
                        y_copy(main(x, yi, p), yi, p, way).start()

                    x_copy(main(x, yi, p), yi, p, 0).start()
                    x_copy(main(x, yi, p), yi, p, 1).start()

    def u_step(step):
        for way in (0, 1):
            yi = y - step if way == 0 else y + step

            @pl.when((yi >= 0) & (yi < NY))
            def _(yi=yi, way=way):
                arrived(bundle(yi), u_recv.at[yi])

                @pl.when(further(way))
                def _():
                    u_copy(yi, way).start()

    def edges_forward():
        edge_arrived(x_prev, 0)
        e_forward(0).start()
        edge_arrived(x_next, 1)
        e_forward(1).start()

    def own_bundle():
        local.wait()
        edge_arrived(x_prev, 1)
        edge_arrived(x_next, 0)
        edge_arrived(x_far, 0)
        edge_arrived(x_far, 1)
        for way in (0, 1):
            @pl.when(further(way))
            def _():
                u_copy(y, way).start()

    order = (
        y,
        jnp.where(y == 0, 1, y - 1),
        jnp.where(y <= 1, 2, jnp.where(y == 2, 3, 1)),
        jnp.where(y <= 1, 3, 0),
    )

    def f_copy(k, way):
        xi = x_prev if way == 0 else x_next
        return main_copy(main(xi, order[k], way), xi, order[k], way, f_send.at[way, k], to_x[way])

    def x_forward(k):
        main_arrived(x_prev, order[k], 0)
        f_copy(k, 0).start()
        main_arrived(x_next, order[k], 1)
        f_copy(k, 1).start()

    def add_block(xi, yi):
        shift = row_at(xi, yi) * 2 + col + 64 - 2 * row - 1
        a_two = jnp.concatenate([a_all[shift % 32], a_all[(shift + 1) % 32]], axis=1)
        for n in range(3):
            cols = pl.ds(n * 256, 256)
            acc[:, cols] += jnp.dot(a_two, b_all[xi, yi, :, cols], preferred_element_type=jnp.float32)

    def multiply(k):
        yi = order[k]
        main_arrived(x_prev, yi, 1)
        main_arrived(x_next, yi, 0)

        @pl.loop(0, 3)
        def _(j):
            add_block((x + NX - 1 + j) % NX, yi)

        main_arrived(x_far, yi, 0)
        main_arrived(x_far, yi, 1)
        add_block(x_far, yi)

    edges_forward()
    a_step(0, 1)
    x_forward(0)
    y_step(1)
    own_bundle()
    a_step(0, 2)
    x_forward(1)
    a_other_half()
    y_step(2)
    a_step(0, 3)
    a_step(1, 1)
    u_step(1)
    x_forward(2)
    y_step(3)
    a_step(0, 4)
    a_step(1, 2)
    u_step(2)
    a_step(1, 3)
    a_step(1, 4)
    for half in range(NH):
        for zi in range(NZ):
            a_arrived(col_at(half, zi, 1 - core))
    multiply(0)
    multiply(1)
    x_forward(3)
    multiply(2)
    u_step(3)
    multiply(3)
    out_ref[...] = acc[...].astype(out_ref.dtype)

    a_copy(a_ref, col, h_send, to_h).wait_send()
    for kind in (0, 1):
        for way in (0, 1):
            for hop in range(a_hops[kind][way]):
                z_copy(a_ref, col, kind, way, hop).wait_send()
        for zi in range(NZ):
            core_copy(a_ref, col, zi, kind).wait_send()
    for way in (0, 1):
        for p in (0, 1):
            e_copy(p, way).wait_send()
        e_forward(way).wait_send()
        for yi in range(NY):
            @pl.when(further(way) & ((yi <= y) if way == 0 else (yi >= y)))
            def _():
                y_copy(own_main(0), yi, 0, way).wait_send()
                y_copy(own_main(1), yi, 1, way).wait_send()
                u_copy(yi, way).wait_send()

            x_copy(own_main(0), yi, 0, way).wait_send()
            x_copy(own_main(1), yi, 1, way).wait_send()
            f_copy(yi, way).wait_send()


def per_device(row_ids, a_tiles, a_mask, b_tiles, b_mask, c_keep):
    def by_blocks(array, blocks):
        wide = jnp.repeat(blocks, TILE, axis=1).astype(array.dtype)
        tall = array.reshape(blocks.shape[0], TILE, array.shape[1])
        return (tall * wide[:, None, :]).reshape(array.shape)

    a_eff = by_blocks(a_tiles, a_mask)
    b_eff = by_blocks(b_tiles, b_mask)
    dma = pltpu.SemaphoreType.DMA
    product = pl.pallas_call(
        kernel,
        out_shape=jax.ShapeDtypeStruct((512, 768), jnp.bfloat16),
        in_specs=[pl.BlockSpec(memory_space=pltpu.VMEM)] * 2,
        out_specs=pl.BlockSpec(memory_space=pltpu.VMEM),
        scratch_shapes=[
            pltpu.VMEM((32, 512, 128), jnp.bfloat16),
            pltpu.VMEM((NX, NY, 256, 768), jnp.bfloat16),
            pltpu.VMEM((512, 768), jnp.float32),
            dma((32,)),
            dma((NX, NY, 2)),
            dma((NX, 2)),
            dma((NY,)),
            dma((16,)),
            dma((2, 2, 4)),
            dma,
            dma((2, NY, 2)),
            dma((2, NY, 2)),
            dma((2, NY)),
            dma((2, 2)),
            dma((2,)),
            dma((2, NY)),
            dma,
        ],
        compiler_params=pltpu.CompilerParams(collective_id=0, has_side_effects=True),
    )(a_eff, b_eff)
    onehot = (row_ids[:, None] == jnp.arange(c_keep.shape[0], dtype=jnp.int32)[None, :]).astype(
        jnp.float32
    )
    keep = jnp.dot(onehot, c_keep.astype(jnp.float32))
    return by_blocks(product, keep)


def solution(mesh):
    placed = (
        P("row"),
        P("row", "col"),
        P("row", "col"),
        P("row", "col"),
        P("row", "col"),
        P(None, "col"),
    )
    return jax.shard_map(
        per_device, mesh=mesh, in_specs=placed, out_specs=P("row", "col"), check_vma=False
    )
```

```python
import jax
import jax.numpy as jnp
from jax import lax
from jax.experimental import pallas as pl
from jax.experimental.pallas import tpu as pltpu
from jax.sharding import PartitionSpec as P

TILE = 64
NX, NY, NH, NZ = 4, 4, 2, 8
MAIN, EDGE = 112, 16
MESH = pl.DeviceIdType.MESH


def kernel(a_hbm, b_hbm, a_mask, b_mask, row_ids, c_keep, out_ref, a_raw, b_raw, a_all, b_all, acc, a_recv, b_recv, e_recv, u_recv, core_send, z_send,
           h_send, y_send, x_send, f_send, e_send, ef_send, u_send, local_sem):
    row = lax.axis_index("row")
    col = lax.axis_index("col")
    x, y = row // NY, row % NY
    core, z, h = col % 2, (col // 2) % NZ, col // (2 * NZ)

    def row_at(xi, yi):
        return xi * NY + yi

    def col_at(hi, zi, ci):
        return (hi * NZ + zi) * 2 + ci

    x_next, x_prev, x_far = (x + 1) % NX, (x + NX - 1) % NX, (x + 2) % NX
    to_x = ((row_at(x_next, y), col), (row_at(x_prev, y), col))
    to_y = ((row_at(x, (y + 1) % NY), col), (row_at(x, (y + NY - 1) % NY), col))
    to_z = ((row, col_at(h, (z + 1) % NZ, core)), (row, col_at(h, (z + NZ - 1) % NZ, core)))
    to_core = (row, col_at(h, z, 1 - core))
    to_h = (row, col_at(1 - h, z, core))

    a_fetch = pltpu.make_async_copy(a_hbm, a_raw, local_sem.at[0])
    b_fetch = pltpu.make_async_copy(b_hbm, b_raw, local_sem.at[1])
    b_fetch.start()
    a_fetch.start()
    barrier = pltpu.get_barrier_semaphore()
    partners = (*to_x, *to_y, *to_z, to_core, to_h)
    for partner in partners:
        pl.semaphore_signal(barrier, inc=1, device_id=partner, device_id_type=MESH)

    left = lax.broadcasted_iota(jnp.int32, (TILE, 2 * TILE), 1) < TILE

    def two_blocks(first, second):
        factor = jnp.where(left, first, second)
        return factor.astype(jnp.float32)

    b_fetch.wait()
    for i in range(4):
        for j in range(6):
            rows, cols = pl.ds(i * TILE, TILE), pl.ds(j * 2 * TILE, 2 * TILE)
            b_all[x, y, rows, cols] = b_raw[rows, cols] * two_blocks(b_mask[i, 2 * j], b_mask[i, 2 * j + 1]).astype(jnp.bfloat16)
    a_fetch.wait()
    for i in range(8):
        rows = pl.ds(i * TILE, TILE)
        a_all[col, rows] = a_raw[rows] * two_blocks(a_mask[0, i], a_mask[1, i]).astype(jnp.bfloat16)
    pl.semaphore_wait(barrier, len(partners))
    acc[...] = jnp.zeros_like(acc)

    def send(source, target, send_sem, recv_sem, to):
        return pltpu.make_async_remote_copy(
            src_ref=source, dst_ref=target, send_sem=send_sem, recv_sem=recv_sem,
            device_id=to, device_id_type=MESH)

    def arrived(target, recv_sem):
        send(target, target, h_send, recv_sem, to_core).wait_recv()

    def a_copy(source, q, send_sem, to):
        return send(source, a_all.at[q], send_sem, a_recv.at[q], to)

    def a_arrived(q):
        arrived(a_all.at[q], a_recv.at[q])

    def main(xi, yi, p):
        return b_all.at[xi, yi, pl.ds(p * MAIN, MAIN)]

    def edge(xi, yi, p):
        return b_all.at[xi, yi, pl.ds(2 * MAIN + p * EDGE, EDGE)]

    def bundle(yi):
        return b_all.at[:, yi, pl.ds(2 * MAIN, 2 * EDGE)]

    def main_copy(source, xi, yi, p, send_sem, to):
        return send(source, main(xi, yi, p), send_sem, b_recv.at[xi, yi, p], to)

    def main_arrived(xi, yi, p):
        arrived(main(xi, yi, p), b_recv.at[xi, yi, p])

    def edge_arrived(xi, p):
        arrived(edge(xi, y, p), e_recv.at[xi, p])

    def own_main(p):
        return main(x, y, p)

    def own_edge(p):
        return edge(x, y, p)

    def y_copy(source, yi, p, way):
        return main_copy(source, x, yi, p, y_send.at[way, yi, p], to_y[way])

    def x_copy(source, yi, p, way):
        return main_copy(source, x, yi, p, x_send.at[way, yi, p], to_x[way])

    def e_copy(p, way):
        return send(own_edge(p), edge(x, y, p), e_send.at[way, p], e_recv.at[x, p], to_x[way])

    def e_forward(way):
        xi = x_prev if way == 0 else x_next
        return send(edge(xi, y, way), edge(xi, y, way), ef_send.at[way], e_recv.at[xi, way], to_x[way])

    def u_copy(yi, way):
        return send(bundle(yi), bundle(yi), u_send.at[way, yi], u_recv.at[yi], to_y[way])

    a_hops = ((4, 3), (3, 4))

    def z_copy(source, q, kind, way, hop):
        return a_copy(source, q, z_send.at[kind, way, hop], to_z[way])

    def core_copy(source, q, zi, kind):
        return a_copy(source, q, core_send.at[kind * NZ + zi], to_core)

    def further(way):
        return (y < NY - 1) if way == 0 else (y > 0)

    a_own = a_all.at[col]
    for p in (0, 1):
        e_copy(p, 0).start()
        e_copy(1 - p, 1).start()
    for p in (0, 1):
        for way in (0, 1):
            @pl.when(further(way))
            def _():
                y_copy(own_main(p), y, p, way).start()

        x_copy(own_main(p), y, p, 0).start()
        x_copy(own_main(1 - p), y, 1 - p, 1).start()
    z_copy(a_own, col, 0, 0, 0).start()
    z_copy(a_own, col, 0, 1, 0).start()
    a_copy(a_own, col, h_send, to_h).start()
    core_copy(a_own, col, z, 0).start()

    def a_step(kind, step):
        half = h if kind == 0 else 1 - h
        for way in (0, 1):
            if step <= a_hops[kind][way]:
                zi = (z + (NZ - step if way == 0 else step)) % NZ
                q = col_at(half, zi, core)
                a_arrived(q)
                if step < a_hops[kind][way]:
                    z_copy(a_all.at[q], q, kind, way, step).start()
                core_copy(a_all.at[q], q, zi, kind).start()

    def a_other_half():
        q = col_at(1 - h, z, core)
        a_arrived(q)
        z_copy(a_all.at[q], q, 1, 0, 0).start()
        z_copy(a_all.at[q], q, 1, 1, 0).start()
        core_copy(a_all.at[q], q, z, 1).start()

    def y_step(step):
        for way in (0, 1):
            yi = y - step if way == 0 else y + step

            @pl.when((yi >= 0) & (yi < NY))
            def _(yi=yi, way=way):
                for p in (0, 1):
                    main_arrived(x, yi, p)

                    @pl.when(further(way))
                    def _():
                        y_copy(main(x, yi, p), yi, p, way).start()

                    x_copy(main(x, yi, p), yi, p, 0).start()
                    x_copy(main(x, yi, p), yi, p, 1).start()

    def u_step(step):
        for way in (0, 1):
            yi = y - step if way == 0 else y + step

            @pl.when((yi >= 0) & (yi < NY))
            def _(yi=yi, way=way):
                arrived(bundle(yi), u_recv.at[yi])

                @pl.when(further(way))
                def _():
                    u_copy(yi, way).start()

    def edges_forward():
        edge_arrived(x_prev, 0)
        e_forward(0).start()
        edge_arrived(x_next, 1)
        e_forward(1).start()

    def own_bundle():
        edge_arrived(x_prev, 1)
        edge_arrived(x_next, 0)
        edge_arrived(x_far, 0)
        edge_arrived(x_far, 1)
        for way in (0, 1):
            @pl.when(further(way))
            def _():
                u_copy(y, way).start()

    order = (
        y,
        jnp.where(y == 0, 1, y - 1),
        jnp.where(y <= 1, 2, jnp.where(y == 2, 3, 1)),
        jnp.where(y <= 1, 3, 0),
    )

    def f_copy(k, way):
        xi = x_prev if way == 0 else x_next
        return main_copy(main(xi, order[k], way), xi, order[k], way, f_send.at[way, k], to_x[way])

    def x_forward(k):
        main_arrived(x_prev, order[k], 0)
        f_copy(k, 0).start()
        main_arrived(x_next, order[k], 1)
        f_copy(k, 1).start()

    def add_block(xi, yi):
        shift = row_at(xi, yi) * 2 + col + 64 - 2 * row - 1
        a_two = jnp.concatenate([a_all[shift % 32], a_all[(shift + 1) % 32]], axis=1)
        for n in range(3):
            cols = pl.ds(n * 256, 256)
            acc[:, cols] += jnp.dot(a_two, b_all[xi, yi, :, cols], preferred_element_type=jnp.float32)

    def multiply(k):
        yi = order[k]
        main_arrived(x_prev, yi, 1)
        main_arrived(x_next, yi, 0)

        @pl.loop(0, 3)
        def _(j):
            add_block((x + NX - 1 + j) % NX, yi)

        main_arrived(x_far, yi, 0)
        main_arrived(x_far, yi, 1)
        add_block(x_far, yi)

    edges_forward()
    a_step(0, 1)
    x_forward(0)
    y_step(1)
    own_bundle()
    a_step(0, 2)
    x_forward(1)
    a_other_half()
    y_step(2)
    a_step(0, 3)
    a_step(1, 1)
    u_step(1)
    x_forward(2)
    y_step(3)
    a_step(0, 4)
    a_step(1, 2)
    u_step(2)
    a_step(1, 3)
    a_step(1, 4)
    for half in range(NH):
        for zi in range(NZ):
            a_arrived(col_at(half, zi, 1 - core))
    x_forward(3)
    u_step(3)
    multiply(0)
    multiply(1)
    multiply(2)
    multiply(3)
    for i in range(8):
        slot = row_ids[i]
        held = jnp.maximum(slot, 0)
        live = jnp.where(slot >= 0, 1, 0)
        for j in range(6):
            rows, cols = pl.ds(i * TILE, TILE), pl.ds(j * 2 * TILE, 2 * TILE)
            keep = jnp.where(left, c_keep[2 * j, held] * live, c_keep[2 * j + 1, held] * live)
            out_ref[rows, cols] = (acc[rows, cols] * keep.astype(jnp.float32)).astype(out_ref.dtype)

    a_copy(a_own, col, h_send, to_h).wait_send()
    for kind in (0, 1):
        for way in (0, 1):
            for hop in range(a_hops[kind][way]):
                z_copy(a_own, col, kind, way, hop).wait_send()
        for zi in range(NZ):
            core_copy(a_own, col, zi, kind).wait_send()
    for way in (0, 1):
        for p in (0, 1):
            e_copy(p, way).wait_send()
        e_forward(way).wait_send()
        for yi in range(NY):
            @pl.when(further(way) & ((yi <= y) if way == 0 else (yi >= y)))
            def _():
                y_copy(own_main(0), yi, 0, way).wait_send()
                y_copy(own_main(1), yi, 1, way).wait_send()
                u_copy(yi, way).wait_send()

            x_copy(own_main(0), yi, 0, way).wait_send()
            x_copy(own_main(1), yi, 1, way).wait_send()
            f_copy(yi, way).wait_send()


def per_device(row_ids, a_tiles, a_mask, b_tiles, b_mask, c_keep):
    dma = pltpu.SemaphoreType.DMA
    product = pl.pallas_call(
        kernel,
        out_shape=jax.ShapeDtypeStruct((512, 768), jnp.bfloat16),
        in_specs=[pl.BlockSpec(memory_space=pl.ANY)] * 2 + [pl.BlockSpec(memory_space=pltpu.SMEM)] * 4,
        out_specs=pl.BlockSpec(memory_space=pltpu.VMEM),
        scratch_shapes=[
            pltpu.VMEM((512, 128), jnp.bfloat16),
            pltpu.VMEM((256, 768), jnp.bfloat16),
            pltpu.VMEM((32, 512, 128), jnp.bfloat16),
            pltpu.VMEM((NX, NY, 256, 768), jnp.bfloat16),
            pltpu.VMEM((512, 768), jnp.float32),
            dma((32,)),
            dma((NX, NY, 2)),
            dma((NX, 2)),
            dma((NY,)),
            dma((16,)),
            dma((2, 2, 4)),
            dma,
            dma((2, NY, 2)),
            dma((2, NY, 2)),
            dma((2, NY)),
            dma((2, 2)),
            dma((2,)),
            dma((2, NY)),
            dma((2,)),
        ],
        compiler_params=pltpu.CompilerParams(collective_id=0, has_side_effects=True),
    )(a_tiles, b_tiles, a_mask.T, b_mask, row_ids, c_keep.T)
    return product


def solution(mesh):
    placed = (
        P("row"),
        P("row", "col"),
        P("row", "col"),
        P("row", "col"),
        P("row", "col"),
        P(None, "col"),
    )
    return jax.shard_map(
        per_device, mesh=mesh, in_specs=placed, out_specs=P("row", "col"), check_vma=False
    )
```

```python
import jax
import jax.numpy as jnp
from jax import lax
from jax.experimental import pallas as pl
from jax.experimental.pallas import tpu as pltpu
from jax.sharding import PartitionSpec as P

TILE = 64
NX, NY, NH, NZ = 4, 4, 2, 8
MAIN, EDGE = ((0, 112), (112, 96)), ((208, 16), (224, 32))
BUNDLE = (208, 48)
MESH = pl.DeviceIdType.MESH


def kernel(a_hbm, b_hbm, am_hbm, bm_hbm, ids_hbm, keep_hbm, out_ref, a_raw, b_raw, a_mask, b_mask, row_ids, c_keep, a_all, b_all, acc, a_recv, b_recv, e_recv, u_recv, core_send, z_send,
           h_send, y_send, x_send, f_send, e_send, ef_send, u_send, local_sem, transit, t_send, t_recv):
    row = lax.axis_index("row")
    col = lax.axis_index("col")
    x, y = row // NY, row % NY
    core, z, h = col % 2, (col // 2) % NZ, col // (2 * NZ)

    def row_at(xi, yi):
        return xi * NY + yi

    def col_at(hi, zi, ci):
        return (hi * NZ + zi) * 2 + ci

    x_next, x_prev, x_far = (x + 1) % NX, (x + NX - 1) % NX, (x + 2) % NX
    to_x = ((row_at(x_next, y), col), (row_at(x_prev, y), col))
    to_y = ((row_at(x, (y + 1) % NY), col), (row_at(x, (y + NY - 1) % NY), col))
    to_z = ((row, col_at(h, (z + 1) % NZ, core)), (row, col_at(h, (z + NZ - 1) % NZ, core)))
    to_core = (row, col_at(h, z, 1 - core))

    ring = 2 * NY
    place, turn = h * NY + y + ring, 1 - 2 * core

    def ring_at(at):
        return (row_at(x, at % NY), col_at((at % ring) // NY, z, core))


    a_fetch = pltpu.make_async_copy(a_hbm, a_raw, local_sem.at[0])
    b_fetch = pltpu.make_async_copy(b_hbm, b_raw, local_sem.at[1])
    am_fetch = pltpu.make_async_copy(am_hbm, a_mask, local_sem.at[2])
    bm_fetch = pltpu.make_async_copy(bm_hbm, b_mask, local_sem.at[3])
    ids_fetch = pltpu.make_async_copy(ids_hbm, row_ids, local_sem.at[4])
    keep_fetch = pltpu.make_async_copy(keep_hbm, c_keep, local_sem.at[5])
    for fetch in (bm_fetch, b_fetch, am_fetch, a_fetch, ids_fetch, keep_fetch):
        fetch.start()
    barrier = pltpu.get_barrier_semaphore()
    partners = (*to_x, *to_z, to_core, *(ring_at(place + hops) for hops in (1, -1, 3, -3)))
    for partner in partners:
        pl.semaphore_signal(barrier, inc=1, device_id=partner, device_id_type=MESH)

    left = lax.broadcasted_iota(jnp.int32, (TILE, 2 * TILE), 1) < TILE

    def two_blocks(first, second):
        factor = jnp.where(left, first, second)
        return factor.astype(jnp.float32)

    bm_fetch.wait()
    b_fetch.wait()
    for i in range(4):
        for j in range(6):
            rows, cols = pl.ds(i * TILE, TILE), pl.ds(j * 2 * TILE, 2 * TILE)
            b_all[x, y, rows, cols] = b_raw[rows, cols] * two_blocks(b_mask[i, 2 * j], b_mask[i, 2 * j + 1]).astype(jnp.bfloat16)
    am_fetch.wait()
    a_fetch.wait()
    for i in range(8):
        rows = pl.ds(i * TILE, TILE)
        a_all[col, rows] = a_raw[rows] * two_blocks(a_mask[0, i], a_mask[1, i]).astype(jnp.bfloat16)
    pl.semaphore_wait(barrier, len(partners))
    acc[...] = jnp.zeros_like(acc)

    def send(source, target, send_sem, recv_sem, to):
        return pltpu.make_async_remote_copy(
            src_ref=source, dst_ref=target, send_sem=send_sem, recv_sem=recv_sem,
            device_id=to, device_id_type=MESH)

    def arrived(target, recv_sem):
        send(target, target, h_send, recv_sem, to_core).wait_recv()

    def a_copy(source, q, send_sem, to):
        return send(source, a_all.at[q], send_sem, a_recv.at[q], to)

    def a_arrived(q):
        arrived(a_all.at[q], a_recv.at[q])

    def main(xi, yi, p):
        return b_all.at[xi, yi, pl.ds(*MAIN[p])]

    def edge(xi, yi, p):
        return b_all.at[xi, yi, pl.ds(*EDGE[p])]

    def bundle(yi):
        return b_all.at[:, yi, pl.ds(*BUNDLE)]

    def main_copy(source, xi, yi, p, send_sem, to):
        return send(source, main(xi, yi, p), send_sem, b_recv.at[xi, yi, p], to)

    def main_arrived(xi, yi, p):
        arrived(main(xi, yi, p), b_recv.at[xi, yi, p])

    def edge_arrived(xi, p):
        arrived(edge(xi, y, p), e_recv.at[xi, p])

    def own_main(p):
        return main(x, y, p)

    def own_edge(p):
        return edge(x, y, p)

    def y_copy(source, yi, p, way):
        return main_copy(source, x, yi, p, y_send.at[way, yi, p], to_y[way])

    def x_copy(source, yi, p, way):
        return main_copy(source, x, yi, p, x_send.at[way, yi, p], to_x[way])

    def e_copy(p, way):
        return send(own_edge(p), edge(x, y, p), e_send.at[way, p], e_recv.at[x, p], to_x[way])

    def e_forward(way):
        xi = x_prev if way == 0 else x_next
        return send(edge(xi, y, way), edge(xi, y, way), ef_send.at[way], e_recv.at[xi, way], to_x[way])

    def u_copy(yi, way):
        return send(bundle(yi), bundle(yi), u_send.at[way, yi], u_recv.at[yi], to_y[way])

    a_hops = ((4, 3), (3, 4))

    def z_copy(source, q, kind, way, hop):
        return a_copy(source, q, z_send.at[kind, way, hop], to_z[way])

    def core_copy(source, q, zi, kind):
        return a_copy(source, q, core_send.at[kind * NZ + zi], to_core)

    def further(way):
        return (y < NY - 1) if way == 0 else (y > 0)

    a_own = a_all.at[col]
    for p in (0, 1):
        e_copy(p, 0).start()
        e_copy(1 - p, 1).start()
    for p in (0, 1):
        for way in (0, 1):
            @pl.when(further(way))
            def _():
                y_copy(own_main(p), y, p, way).start()

        x_copy(own_main(p), y, p, 0).start()
        x_copy(own_main(1 - p), y, 1 - p, 1).start()
    z_copy(a_own, col, 0, 0, 0).start()
    z_copy(a_own, col, 0, 1, 0).start()
    send(a_own, transit, h_send, t_recv, ring_at(place + turn)).start()
    core_copy(a_own, col, z, 0).start()

    def a_step(kind, step):
        half = h if kind == 0 else 1 - h
        for way in (0, 1):
            if step <= a_hops[kind][way]:
                zi = (z + (NZ - step if way == 0 else step)) % NZ
                q = col_at(half, zi, core)
                a_arrived(q)
                if step < a_hops[kind][way]:
                    z_copy(a_all.at[q], q, kind, way, step).start()
                core_copy(a_all.at[q], q, zi, kind).start()

    def relay():
        q = col_at(((place - turn) % ring) // NY, z, core)
        return a_copy(transit, q, t_send, ring_at(place + 3 * turn))

    def a_other_half():
        q = col_at(1 - h, z, core)
        a_arrived(q)
        z_copy(a_all.at[q], q, 1, 0, 0).start()
        z_copy(a_all.at[q], q, 1, 1, 0).start()
        core_copy(a_all.at[q], q, z, 1).start()

    def y_step(step):
        for way in (0, 1):
            yi = y - step if way == 0 else y + step

            @pl.when((yi >= 0) & (yi < NY))
            def _(yi=yi, way=way):
                for p in (0, 1):
                    main_arrived(x, yi, p)

                    @pl.when(further(way))
                    def _():
                        y_copy(main(x, yi, p), yi, p, way).start()

                    x_copy(main(x, yi, p), yi, p, 0).start()
                    x_copy(main(x, yi, p), yi, p, 1).start()

    def u_step(step):
        for way in (0, 1):
            yi = y - step if way == 0 else y + step

            @pl.when((yi >= 0) & (yi < NY))
            def _(yi=yi, way=way):
                arrived(bundle(yi), u_recv.at[yi])

                @pl.when(further(way))
                def _():
                    u_copy(yi, way).start()

    def edges_forward():
        edge_arrived(x_prev, 0)
        e_forward(0).start()
        edge_arrived(x_next, 1)
        e_forward(1).start()

    def own_bundle():
        edge_arrived(x_prev, 1)
        edge_arrived(x_next, 0)
        edge_arrived(x_far, 0)
        edge_arrived(x_far, 1)
        for way in (0, 1):
            @pl.when(further(way))
            def _():
                u_copy(y, way).start()

    order = (
        y,
        jnp.where(y == 0, 1, y - 1),
        jnp.where(y <= 1, 2, jnp.where(y == 2, 3, 1)),
        jnp.where(y <= 1, 3, 0),
    )

    def f_copy(k, way):
        xi = x_prev if way == 0 else x_next
        return main_copy(main(xi, order[k], way), xi, order[k], way, f_send.at[way, k], to_x[way])

    def x_forward(k):
        main_arrived(x_prev, order[k], 0)
        f_copy(k, 0).start()
        main_arrived(x_next, order[k], 1)
        f_copy(k, 1).start()

    def add_block(xi, yi):
        shift = row_at(xi, yi) * 2 + col + 64 - 2 * row - 1
        a_two = jnp.concatenate([a_all[shift % 32], a_all[(shift + 1) % 32]], axis=1)
        for n in range(3):
            cols = pl.ds(n * 256, 256)
            acc[:, cols] += jnp.dot(a_two, b_all[xi, yi, :, cols], preferred_element_type=jnp.float32)

    def multiply(k):
        yi = order[k]
        main_arrived(x_prev, yi, 1)
        main_arrived(x_next, yi, 0)

        @pl.loop(0, 3)
        def _(j):
            add_block((x + NX - 1 + j) % NX, yi)

        main_arrived(x_far, yi, 0)
        main_arrived(x_far, yi, 1)
        add_block(x_far, yi)

    edges_forward()
    a_step(0, 1)
    x_forward(0)
    y_step(1)
    arrived(transit, t_recv)
    relay().start()
    own_bundle()
    a_step(0, 2)
    x_forward(1)
    a_other_half()
    y_step(2)
    a_step(0, 3)
    a_step(1, 1)
    u_step(1)
    x_forward(2)
    y_step(3)
    a_step(0, 4)
    a_step(1, 2)
    u_step(2)
    a_step(1, 3)
    a_step(1, 4)
    for half in range(NH):
        for zi in range(NZ):
            a_arrived(col_at(half, zi, 1 - core))
    x_forward(3)
    u_step(3)
    multiply(0)
    multiply(1)
    multiply(2)
    multiply(3)
    ids_fetch.wait()
    keep_fetch.wait()
    for i in range(8):
        slot = row_ids[i]
        held = jnp.maximum(slot, 0)
        live = jnp.where(slot >= 0, 1, 0)
        for j in range(6):
            rows, cols = pl.ds(i * TILE, TILE), pl.ds(j * 2 * TILE, 2 * TILE)
            keep = jnp.where(left, c_keep[2 * j, held] * live, c_keep[2 * j + 1, held] * live)
            out_ref[rows, cols] = (acc[rows, cols] * keep.astype(jnp.float32)).astype(out_ref.dtype)

    send(a_own, transit, h_send, t_recv, ring_at(place + turn)).wait_send()
    relay().wait_send()
    for kind in (0, 1):
        for way in (0, 1):
            for hop in range(a_hops[kind][way]):
                z_copy(a_own, col, kind, way, hop).wait_send()
        for zi in range(NZ):
            core_copy(a_own, col, zi, kind).wait_send()
    for way in (0, 1):
        for p in (0, 1):
            e_copy(p, way).wait_send()
        e_forward(way).wait_send()
        for yi in range(NY):
            @pl.when(further(way) & ((yi <= y) if way == 0 else (yi >= y)))
            def _():
                y_copy(own_main(0), yi, 0, way).wait_send()
                y_copy(own_main(1), yi, 1, way).wait_send()
                u_copy(yi, way).wait_send()

            x_copy(own_main(0), yi, 0, way).wait_send()
            x_copy(own_main(1), yi, 1, way).wait_send()
            f_copy(yi, way).wait_send()


def per_device(row_ids, a_tiles, a_mask, b_tiles, b_mask, c_keep):
    dma = pltpu.SemaphoreType.DMA
    product = pl.pallas_call(
        kernel,
        out_shape=jax.ShapeDtypeStruct((512, 768), jnp.bfloat16),
        in_specs=[pl.BlockSpec(memory_space=pltpu.HBM)] * 6,
        out_specs=pl.BlockSpec(memory_space=pltpu.VMEM),
        scratch_shapes=[
            pltpu.VMEM((512, 128), jnp.bfloat16),
            pltpu.VMEM((256, 768), jnp.bfloat16),
            pltpu.SMEM((2, 8), jnp.int32),
            pltpu.SMEM((4, 12), jnp.int32),
            pltpu.SMEM((8,), jnp.int32),
            pltpu.SMEM((12, 128), jnp.int32),
            pltpu.VMEM((32, 512, 128), jnp.bfloat16),
            pltpu.VMEM((NX, NY, 256, 768), jnp.bfloat16),
            pltpu.VMEM((512, 768), jnp.float32),
            dma((32,)),
            dma((NX, NY, 2)),
            dma((NX, 2)),
            dma((NY,)),
            dma((16,)),
            dma((2, 2, 4)),
            dma,
            dma((2, NY, 2)),
            dma((2, NY, 2)),
            dma((2, NY)),
            dma((2, 2)),
            dma((2,)),
            dma((2, NY)),
            dma((6,)),
            pltpu.VMEM((512, 128), jnp.bfloat16),
            dma,
            dma,
        ],
        compiler_params=pltpu.CompilerParams(collective_id=0, has_side_effects=True),
    )(a_tiles, b_tiles, a_mask.T, b_mask, row_ids, c_keep.T)
    return product


def solution(mesh):
    placed = (
        P("row"),
        P("row", "col"),
        P("row", "col"),
        P("row", "col"),
        P("row", "col"),
        P(None, "col"),
    )
    return jax.shard_map(
        per_device, mesh=mesh, in_specs=placed, out_specs=P("row", "col"), check_vma=False
    )
```

```python
import jax
import jax.numpy as jnp
from jax import lax
from jax.experimental import pallas as pl
from jax.experimental.pallas import tpu as pltpu
from jax.sharding import PartitionSpec as P

TILE = 64
NX, NY, NH, NZ = 4, 4, 2, 8
MAIN, EDGE = 112, 16
MESH = pl.DeviceIdType.MESH


def kernel(a_hbm, b_hbm, am_hbm, bm_hbm, ids_hbm, keep_hbm, out_ref, a_raw, b_raw, a_mask, b_mask, row_ids, c_keep, a_all, b_all, acc, a_recv, b_recv, e_recv, u_recv, core_send, z_send,
           h_send, y_send, x_send, f_send, e_send, ef_send, u_send, local_sem):
    row = lax.axis_index("row")
    col = lax.axis_index("col")
    x, y = row // NY, row % NY
    core, z, h = col % 2, (col // 2) % NZ, col // (2 * NZ)

    def row_at(xi, yi):
        return xi * NY + yi

    def col_at(hi, zi, ci):
        return (hi * NZ + zi) * 2 + ci

    x_next, x_prev, x_far = (x + 1) % NX, (x + NX - 1) % NX, (x + 2) % NX
    to_x = ((row_at(x_next, y), col), (row_at(x_prev, y), col))
    to_y = ((row_at(x, (y + 1) % NY), col), (row_at(x, (y + NY - 1) % NY), col))
    to_z = ((row, col_at(h, (z + 1) % NZ, core)), (row, col_at(h, (z + NZ - 1) % NZ, core)))
    to_core = (row, col_at(h, z, 1 - core))
    to_h = (row, col_at(1 - h, z, core))

    a_fetch = pltpu.make_async_copy(a_hbm, a_raw, local_sem.at[0])
    b_fetch = pltpu.make_async_copy(b_hbm, b_raw, local_sem.at[1])
    am_fetch = pltpu.make_async_copy(am_hbm, a_mask, local_sem.at[2])
    bm_fetch = pltpu.make_async_copy(bm_hbm, b_mask, local_sem.at[3])
    ids_fetch = pltpu.make_async_copy(ids_hbm, row_ids, local_sem.at[4])
    keep_fetch = pltpu.make_async_copy(keep_hbm, c_keep, local_sem.at[5])
    for fetch in (bm_fetch, b_fetch, am_fetch, a_fetch, ids_fetch, keep_fetch):
        fetch.start()
    barrier = pltpu.get_barrier_semaphore()
    partners = (*to_x, *to_y, *to_z, to_core, to_h)
    for partner in partners:
        pl.semaphore_signal(barrier, inc=1, device_id=partner, device_id_type=MESH)

    left = lax.broadcasted_iota(jnp.int32, (TILE, 2 * TILE), 1) < TILE

    def two_blocks(first, second):
        factor = jnp.where(left, first, second)
        return factor.astype(jnp.float32)

    bm_fetch.wait()
    b_fetch.wait()
    for i in range(4):
        for j in range(6):
            rows, cols = pl.ds(i * TILE, TILE), pl.ds(j * 2 * TILE, 2 * TILE)
            b_all[x, y, rows, cols] = b_raw[rows, cols] * two_blocks(b_mask[i, 2 * j], b_mask[i, 2 * j + 1]).astype(jnp.bfloat16)
    am_fetch.wait()
    a_fetch.wait()
    for i in range(8):
        rows = pl.ds(i * TILE, TILE)
        a_all[col, rows] = a_raw[rows] * two_blocks(a_mask[0, i], a_mask[1, i]).astype(jnp.bfloat16)
    pl.semaphore_wait(barrier, len(partners))
    acc[...] = jnp.zeros_like(acc)

    def send(source, target, send_sem, recv_sem, to):
        return pltpu.make_async_remote_copy(
            src_ref=source, dst_ref=target, send_sem=send_sem, recv_sem=recv_sem,
            device_id=to, device_id_type=MESH)

    def arrived(target, recv_sem):
        send(target, target, h_send, recv_sem, to_core).wait_recv()

    def a_copy(source, q, send_sem, to):
        return send(source, a_all.at[q], send_sem, a_recv.at[q], to)

    def a_arrived(q):
        arrived(a_all.at[q], a_recv.at[q])

    def main(xi, yi, p):
        return b_all.at[xi, yi, pl.ds(p * MAIN, MAIN)]

    def edge(xi, yi, p):
        return b_all.at[xi, yi, pl.ds(2 * MAIN + p * EDGE, EDGE)]

    def bundle(yi):
        return b_all.at[:, yi, pl.ds(2 * MAIN, 2 * EDGE)]

    def main_copy(source, xi, yi, p, send_sem, to):
        return send(source, main(xi, yi, p), send_sem, b_recv.at[xi, yi, p], to)

    def main_arrived(xi, yi, p):
        arrived(main(xi, yi, p), b_recv.at[xi, yi, p])

    def edge_arrived(xi, p):
        arrived(edge(xi, y, p), e_recv.at[xi, p])

    def own_main(p):
        return main(x, y, p)

    def own_edge(p):
        return edge(x, y, p)

    def y_copy(source, yi, p, way):
        return main_copy(source, x, yi, p, y_send.at[way, yi, p], to_y[way])

    def x_copy(source, yi, p, way):
        return main_copy(source, x, yi, p, x_send.at[way, yi, p], to_x[way])

    def e_copy(p, way):
        return send(own_edge(p), edge(x, y, p), e_send.at[way, p], e_recv.at[x, p], to_x[way])

    def e_forward(way):
        xi = x_prev if way == 0 else x_next
        return send(edge(xi, y, way), edge(xi, y, way), ef_send.at[way], e_recv.at[xi, way], to_x[way])

    def u_copy(yi, way):
        return send(bundle(yi), bundle(yi), u_send.at[way, yi], u_recv.at[yi], to_y[way])

    a_hops = ((4, 3), (3, 4))

    def z_copy(source, q, kind, way, hop):
        return a_copy(source, q, z_send.at[kind, way, hop], to_z[way])

    def core_copy(source, q, zi, kind):
        return a_copy(source, q, core_send.at[kind * NZ + zi], to_core)

    def further(way):
        return (y < NY - 1) if way == 0 else (y > 0)

    a_own = a_all.at[col]
    for p in (0, 1):
        e_copy(p, 0).start()
        e_copy(1 - p, 1).start()
    for p in (0, 1):
        for way in (0, 1):
            @pl.when(further(way))
            def _():
                y_copy(own_main(p), y, p, way).start()

        x_copy(own_main(p), y, p, 0).start()
        x_copy(own_main(1 - p), y, 1 - p, 1).start()
    z_copy(a_own, col, 0, 0, 0).start()
    z_copy(a_own, col, 0, 1, 0).start()
    a_copy(a_own, col, h_send, to_h).start()
    core_copy(a_own, col, z, 0).start()

    def a_step(kind, step):
        half = h if kind == 0 else 1 - h
        for way in (0, 1):
            if step <= a_hops[kind][way]:
                zi = (z + (NZ - step if way == 0 else step)) % NZ
                q = col_at(half, zi, core)
                a_arrived(q)
                if step < a_hops[kind][way]:
                    z_copy(a_all.at[q], q, kind, way, step).start()
                core_copy(a_all.at[q], q, zi, kind).start()

    def a_other_half():
        q = col_at(1 - h, z, core)
        a_arrived(q)
        z_copy(a_all.at[q], q, 1, 0, 0).start()
        z_copy(a_all.at[q], q, 1, 1, 0).start()
        core_copy(a_all.at[q], q, z, 1).start()

    def y_step(step):
        for way in (0, 1):
            yi = y - step if way == 0 else y + step

            @pl.when((yi >= 0) & (yi < NY))
            def _(yi=yi, way=way):
                for p in (0, 1):
                    main_arrived(x, yi, p)

                    @pl.when(further(way))
                    def _():
                        y_copy(main(x, yi, p), yi, p, way).start()

                    x_copy(main(x, yi, p), yi, p, 0).start()
                    x_copy(main(x, yi, p), yi, p, 1).start()

    def u_step(step):
        for way in (0, 1):
            yi = y - step if way == 0 else y + step

            @pl.when((yi >= 0) & (yi < NY))
            def _(yi=yi, way=way):
                arrived(bundle(yi), u_recv.at[yi])

                @pl.when(further(way))
                def _():
                    u_copy(yi, way).start()

    def edges_forward():
        edge_arrived(x_prev, 0)
        e_forward(0).start()
        edge_arrived(x_next, 1)
        e_forward(1).start()

    def own_bundle():
        edge_arrived(x_prev, 1)
        edge_arrived(x_next, 0)
        edge_arrived(x_far, 0)
        edge_arrived(x_far, 1)
        for way in (0, 1):
            @pl.when(further(way))
            def _():
                u_copy(y, way).start()

    order = (
        y,
        jnp.where(y == 0, 1, y - 1),
        jnp.where(y <= 1, 2, jnp.where(y == 2, 3, 1)),
        jnp.where(y <= 1, 3, 0),
    )

    def f_copy(k, way):
        xi = x_prev if way == 0 else x_next
        return main_copy(main(xi, order[k], way), xi, order[k], way, f_send.at[way, k], to_x[way])

    def x_forward(k):
        main_arrived(x_prev, order[k], 0)
        f_copy(k, 0).start()
        main_arrived(x_next, order[k], 1)
        f_copy(k, 1).start()

    def add_block(xi, yi):
        shift = row_at(xi, yi) * 2 + col + 64 - 2 * row - 1
        a_two = jnp.concatenate([a_all[shift % 32], a_all[(shift + 1) % 32]], axis=1)
        for n in range(3):
            cols = pl.ds(n * 256, 256)
            acc[:, cols] += jnp.dot(a_two, b_all[xi, yi, :, cols], preferred_element_type=jnp.float32)

    def multiply(k):
        yi = order[k]
        main_arrived(x_prev, yi, 1)
        main_arrived(x_next, yi, 0)

        @pl.loop(0, 3)
        def _(j):
            add_block((x + NX - 1 + j) % NX, yi)

        main_arrived(x_far, yi, 0)
        main_arrived(x_far, yi, 1)
        add_block(x_far, yi)

    edges_forward()
    x_forward(0)
    a_step(0, 1)
    y_step(1)
    own_bundle()
    x_forward(1)
    a_step(0, 2)
    a_other_half()
    y_step(2)
    a_step(0, 3)
    a_step(1, 1)
    u_step(1)
    x_forward(2)
    y_step(3)
    a_step(0, 4)
    a_step(1, 2)
    u_step(2)
    a_step(1, 3)
    a_step(1, 4)
    for half in range(NH):
        for zi in range(NZ):
            a_arrived(col_at(half, zi, 1 - core))
    x_forward(3)
    u_step(3)
    multiply(0)
    multiply(1)
    multiply(2)
    multiply(3)
    ids_fetch.wait()
    keep_fetch.wait()
    for i in range(8):
        slot = row_ids[i]
        held = jnp.maximum(slot, 0)
        live = jnp.where(slot >= 0, 1, 0)
        for j in range(6):
            rows, cols = pl.ds(i * TILE, TILE), pl.ds(j * 2 * TILE, 2 * TILE)
            keep = jnp.where(left, c_keep[2 * j, held] * live, c_keep[2 * j + 1, held] * live)
            out_ref[rows, cols] = (acc[rows, cols] * keep.astype(jnp.float32)).astype(out_ref.dtype)

    a_copy(a_own, col, h_send, to_h).wait_send()
    for kind in (0, 1):
        for way in (0, 1):
            for hop in range(a_hops[kind][way]):
                z_copy(a_own, col, kind, way, hop).wait_send()
        for zi in range(NZ):
            core_copy(a_own, col, zi, kind).wait_send()
    for way in (0, 1):
        for p in (0, 1):
            e_copy(p, way).wait_send()
        e_forward(way).wait_send()
        for yi in range(NY):
            @pl.when(further(way) & ((yi <= y) if way == 0 else (yi >= y)))
            def _():
                y_copy(own_main(0), yi, 0, way).wait_send()
                y_copy(own_main(1), yi, 1, way).wait_send()
                u_copy(yi, way).wait_send()

            x_copy(own_main(0), yi, 0, way).wait_send()
            x_copy(own_main(1), yi, 1, way).wait_send()
            f_copy(yi, way).wait_send()


def per_device(row_ids, a_tiles, a_mask, b_tiles, b_mask, c_keep):
    dma = pltpu.SemaphoreType.DMA
    product = pl.pallas_call(
        kernel,
        out_shape=jax.ShapeDtypeStruct((512, 768), jnp.bfloat16),
        in_specs=[pl.BlockSpec(memory_space=pltpu.HBM)] * 6,
        out_specs=pl.BlockSpec(memory_space=pltpu.VMEM),
        scratch_shapes=[
            pltpu.VMEM((512, 128), jnp.bfloat16),
            pltpu.VMEM((256, 768), jnp.bfloat16),
            pltpu.SMEM((2, 8), jnp.int32),
            pltpu.SMEM((4, 12), jnp.int32),
            pltpu.SMEM((8,), jnp.int32),
            pltpu.SMEM((12, 128), jnp.int32),
            pltpu.VMEM((32, 512, 128), jnp.bfloat16),
            pltpu.VMEM((NX, NY, 256, 768), jnp.bfloat16),
            pltpu.VMEM((512, 768), jnp.float32),
            dma((32,)),
            dma((NX, NY, 2)),
            dma((NX, 2)),
            dma((NY,)),
            dma((16,)),
            dma((2, 2, 4)),
            dma,
            dma((2, NY, 2)),
            dma((2, NY, 2)),
            dma((2, NY)),
            dma((2, 2)),
            dma((2,)),
            dma((2, NY)),
            dma((6,)),
        ],
        compiler_params=pltpu.CompilerParams(collective_id=0, has_side_effects=True),
    )(a_tiles, b_tiles, a_mask.T, b_mask, row_ids, c_keep.T)
    return product


def solution(mesh):
    placed = (
        P("row"),
        P("row", "col"),
        P("row", "col"),
        P("row", "col"),
        P("row", "col"),
        P(None, "col"),
    )
    return jax.shard_map(
        per_device, mesh=mesh, in_specs=placed, out_specs=P("row", "col"), check_vma=False
    )
```
